32 devices in a mesh: groups: 2 (over y), hid: 8 (over z, x), row: 2 (over core).
Axes of the slice: x: 2, y: 2, z: 4, core: 2. Of those that a mesh axis runs over, the one named last changes fastest.
Arguments:
- gate_proj: bfloat16 [32, 32768], P(('groups', 'row'), 'hid'), parts along dimension 0, may hold values from -6 to 6
- up_proj: bfloat16 [32, 32768], P(('groups', 'row'), 'hid'), parts along dimension 0, may hold values from -6 to 6
- hadamard_signs: int32 [32768], P('hid'), may hold values from 0 to 1
- down_codes: bfloat16 [32768, 8192], P('hid', 'row'), may hold values from -127 to 127, as said below
- down_scales: int32 [8192], P('row'), may hold values from 128 to 1279
- residual: bfloat16 [32, 8192], P(('groups', 'hid'), 'row'), parts along dimension 0, may hold values from -16 to 16
- norm_gain: bfloat16 [8192], P('row'), may hold values from 0.099609375 to 1.8984375
- qkv_codes: bfloat16 [8192, 18432], P('row', 'hid'), may hold values from -127 to 127, as said below
- qkv_scales: int32 [18432], P('hid'), may hold values from 128 to 1279
Outputs:
- new_stream: bfloat16 [32, 8192], P(('groups', 'hid'), 'row'), parts along dimension 0
- joined_qkv: bfloat16 [32, 18432], P(('groups', 'row'), 'hid'), parts along dimension 0
The draws below stay inside these ranges and needn't reach their ends.
There are 2 independent parts, one for each index of `groups`. The reference program is written for one: setup_inputs(seed, part) draws one part's arguments, and reference() takes and returns one part's arrays. A program takes and returns all parts, laid end to end along the dimension named above; an argument that names none is the same for every part. Nothing has to cross between parts.
Inputs may be any that keep to these rules, and one draw needn't show every extreme that they name: `down_codes`: every entry is a whole number. `qkv_codes`: every entry is a whole number.
All inputs are finite; a program needn't handle non-finite values.
Results may differ from the reference program's by a relative error of at most 0.0062.
Values may be sent and summed in bfloat16 or wider, within the bound.
A program may use at most 128 MiB of HBM per device.

```python
import math
import jax
import jax.numpy as jnp
from jax import lax

D = 8192
FF = 32768
QKV = 18432
ROWS = 16


def draw_down_codes(key, part):
    return jax.random.randint(jax.random.fold_in(key, 11), (FF, D), -127, 128).astype(jnp.float32).astype(jnp.bfloat16)


def draw_qkv_codes(key, part):
    return jax.random.randint(jax.random.fold_in(key, 23), (D, QKV), -127, 128).astype(jnp.float32).astype(jnp.bfloat16)


def draw_residual(key, part):
    base_key = jax.random.fold_in(key, 37)
    key_noise, key_column = jax.random.split(base_key, 2)
    column_rise = 0.3 * 3.0 ** (jnp.arange(D, dtype=jnp.float32) / D)
    column_spread = jnp.exp(jax.random.uniform(key_column, (D,), jnp.float32, 0.0, math.log(3.3)))
    noise_part = jax.random.truncated_normal(key_noise, -4.0, 4.0, (ROWS, D), jnp.float32)
    values = noise_part * (column_rise * column_spread)[None, :]
    return jnp.clip(values, -16.0, 16.0).astype(jnp.bfloat16)


def place_ends(array, key, smallest, largest):
    place = [jax.random.randint(jax.random.fold_in(key, axis), (), 0, length) for axis, length in enumerate(array.shape)]
    main_axis = array.shape.index(max(array.shape))
    neighbour = place[:main_axis] + [(place[main_axis] + 1) % array.shape[main_axis]] + place[main_axis + 1:]
    return array.at[tuple(place)].set(smallest).at[tuple(neighbour)].set(largest)


def steps_of(own_key, dims, cuts, low, top_value):
    gain = 1.0
    for axis_at, shards_of in cuts:
        steps = jax.random.uniform(jax.random.fold_in(jax.random.fold_in(own_key, 6), axis_at), (shards_of,), jnp.float32, low / len(cuts), top_value / len(cuts))
        gain = gain * jnp.repeat(jnp.exp(steps), dims[axis_at] // shards_of).reshape((-1,) + (1,) * (len(dims) - 1 - axis_at))
    return gain


def normal_values(stream_key, shape, spread, limit, shards=(), held_as=jnp.bfloat16):
    values = jax.random.normal(stream_key, shape, jnp.float32) * spread
    if len(shards) > 0:
        values = steps_of(stream_key, shape, shards, -0.22, 0.18) * values
    return jnp.clip(values, min=-limit, max=limit).astype(held_as)


def setup_inputs(seed: int = 0, part: int = 0) -> dict:
    arg_keys = jax.random.split(jax.random.key(seed), 10)
    part_splits = jax.random.split(jax.random.fold_in(arg_keys[9], part), 10)
    gate_proj = normal_values(part_splits[0], (ROWS, FF), 1.0, 6.0, ((0, 2), (1, 8)))
    up_proj = normal_values(part_splits[1], (ROWS, FF), 1.0, 6.0, ((0, 2), (1, 8)))
    hadamard_signs = place_ends(jax.random.randint(arg_keys[2], (FF,), 0, 2), jax.random.fold_in(arg_keys[2], 1), 0, 1).astype(jnp.int32)
    down_codes = draw_down_codes(jax.random.fold_in(arg_keys[9], 71), part)
    down_scales = place_ends(jax.random.randint(arg_keys[4], (D,), 128, 1280), jax.random.fold_in(arg_keys[4], 1), 128, 1279).astype(jnp.int32)
    residual = draw_residual(jax.random.fold_in(jax.random.fold_in(arg_keys[9], part), 71), part)
    norm_gain = jnp.clip(1.0 + 0.18 * jax.random.normal(arg_keys[6], (D,), jnp.float32), 0.099609375, 1.8984375).astype(jnp.bfloat16)
    qkv_codes = draw_qkv_codes(jax.random.fold_in(arg_keys[9], 71), part)
    qkv_scales = place_ends(jax.random.randint(arg_keys[8], (QKV,), 128, 1280), jax.random.fold_in(arg_keys[8], 1), 128, 1279).astype(jnp.int32)
    return {"gate_proj": gate_proj, "up_proj": up_proj, "hadamard_signs": hadamard_signs, "down_codes": down_codes, "down_scales": down_scales, "residual": residual, "norm_gain": norm_gain, "qkv_codes": qkv_codes, "qkv_scales": qkv_scales}


def sylvester(order_size):
    row_index = lax.broadcasted_iota(jnp.int32, (order_size, order_size), 0)
    column_index = lax.broadcasted_iota(jnp.int32, (order_size, order_size), 1)
    result = jnp.ones((order_size, order_size), jnp.float32)
    for bit_number in range(order_size.bit_length() - 1):
        both_set = row_index // 2 ** bit_number % 2 * (column_index // 2 ** bit_number % 2)
        result = result * (1.0 - 2.0 * both_set.astype(jnp.float32))
    return result

def factor_list(length):
    factors = []
    remain = length
    while remain > 1:
        factor = min(remain, 128)
        factors.append(factor)
        remain = remain // factor
    return factors

def transform_axis(values, order_size, axis_place):
    if order_size == 1:
        return values
    product_moved = jnp.tensordot(values, sylvester(order_size), axes=([axis_place], [0]), precision=lax.Precision.HIGHEST)
    return jnp.moveaxis(product_moved, -1, axis_place)

def transform_last(values):
    factors = factor_list(values.shape[-1])
    leading = values.shape[:-1]
    shaped = values.reshape(leading + tuple(factors))
    for offset, order_size in enumerate(factors):
        shaped = transform_axis(shaped, order_size, len(leading) + offset)
    return shaped.reshape(values.shape)

def reference(gate_proj, up_proj, hadamard_signs, down_codes, down_scales, residual, norm_gain, qkv_codes, qkv_scales):
    hidden = (jax.nn.silu(gate_proj.astype(jnp.float32)) * up_proj.astype(jnp.float32)).astype(jnp.bfloat16)
    flips = (1 - 2 * hadamard_signs).astype(jnp.bfloat16)
    signed = hidden * flips[None, :]
    rotated = (transform_last(signed.astype(jnp.float32)) * (1.0 / math.sqrt(FF))).astype(jnp.bfloat16)
    down = jnp.dot(rotated, down_codes, preferred_element_type=jnp.float32)
    down = down * (down_scales.astype(jnp.float32) * 2.0 ** (-23))[None, :]
    new_stream = (residual.astype(jnp.float32) + down).astype(jnp.bfloat16)
    stream_wide = new_stream.astype(jnp.float32)
    squares = lax.optimization_barrier(jnp.sum(stream_wide * stream_wide, axis=1))
    scaled_rows = (stream_wide * norm_gain.astype(jnp.float32)[None, :]).astype(jnp.bfloat16)
    projected = jnp.dot(scaled_rows, qkv_codes, preferred_element_type=jnp.float32)
    inverse = lax.rsqrt(squares / D + 1e-05)
    joined_qkv = (projected * inverse[:, None] * (qkv_scales.astype(jnp.float32) * 2.0 ** (-22))[None, :]).astype(jnp.bfloat16)
    return (new_stream, joined_qkv)
```

```python
import functools
import math

import jax
import jax.numpy as jnp
from jax import lax
from jax.experimental import pallas as pl
from jax.experimental.pallas import tpu as pltpu
from jax.sharding import PartitionSpec as P

epsilon = 1e-05
F32 = jnp.float32
BF16 = jnp.bfloat16
MESH = pl.DeviceIdType.MESH


def each(count, step, start=0):
    if count - start <= 16:
        for index in range(start, count):
            step(index)
    else:

        def looped(index, carry):
            step(index)
            return carry

        lax.fori_loop(start, count, looped, 0)


def loop(count, step):
    def looped(index, carry):
        step(index)
        return carry

    lax.fori_loop(0, count, looped, 0)


def sylvester(order):
    both = lax.broadcasted_iota(jnp.int32, (order, order), 0) & lax.broadcasted_iota(
        jnp.int32, (order, order), 1
    )
    shift = 1
    while shift < order.bit_length():
        shift *= 2
    while shift > 1:
        shift //= 2
        both = both ^ lax.shift_right_logical(both, shift)
    return (1 - 2 * (both & 1)).astype(F32).astype(BF16)


def tile_of(width, largest):
    tile = largest // 128 * 128
    while width % tile:
        tile -= 128
    return tile


def butterfly(parts):
    step = 1
    while step < len(parts):
        parts = [
            parts[i] + parts[i + step] if i & step == 0 else parts[i - step] - parts[i]
            for i in range(len(parts))
        ]
        step *= 2
    return parts


def kernel(
    A, B, J, M, lo, width_total,
    gate_h, up_h, signs_h, wd_h, dscale_h, res_h, gain_h, wq_h, qscale_h,
    ns_o, out_o,
    gate, up, signs, dscale, res, gain1, qscale, wd, wq, gain,
    send1, recv1, recvr, resf, send2, recv2, lhsf, lhs, send3, recv3, send4, recv4, rowsf, lhs2,
    sq, proj, send5, recv5,
    in_sem, wd_sem, wq_sem, s1, r1, sr, rr, s2, r2, s3, r3, s4, r4, s5, r5,
):
    h = lax.axis_index("hid")
    r = lax.axis_index("row")
    N = A * B
    me = h * B + r
    mine = h - lo
    owner = (h >= lo) & (h < lo + M)
    Rl, FFl = gate.shape
    q = Rl // M
    R = Rl * B
    S = res.shape[0]
    T = R // M
    G = A // M
    C = wd.shape[2]
    Q = wq.shape[2]

    small = [
        pltpu.make_async_copy(src, dst, in_sem.at[k])
        for k, (src, dst) in enumerate(
            [(gate_h, gate), (up_h, up), (signs_h, signs), (res_h, res), (dscale_h, dscale),
             (gain_h, gain1), (qscale_h, qscale)]
        )
    ]
    for copy in small:
        copy.start()

    def wd_copy(j):
        return pltpu.make_async_copy(
            wd_h.at[:, pl.ds(pl.multiple_of(j * C, C), C)], wd.at[j], wd_sem.at[j]
        )

    def wq_copy(j):
        return pltpu.make_async_copy(
            wq_h.at[pl.ds(pl.multiple_of(j * C, C), C), :], wq.at[j], wq_sem.at[j]
        )

    for j in range(J):
        wd_copy(j).start(priority=1)

    barrier = pltpu.get_barrier_semaphore()

    def greet(t):
        peer = lax.rem(me + t, N)
        d = lax.div(peer, B)

        @pl.when(owner | ((d >= lo) & (d < lo + M)) | (d == h))
        def _():
            pl.semaphore_signal(
                barrier, inc=1, device_id={"hid": d, "row": lax.rem(peer, B)}, device_id_type=MESH
            )

    each(N, greet, 1)

    def but_mine(count, first, step):
        def guarded(index):
            @pl.when(first + index != h)
            def _():
                step(index)

        each(count, guarded)

    W = 256
    pieces = FFl // W
    order = sylvester(W)
    for copy in small[:3]:
        copy.wait()
    v = gate[...].astype(F32)
    hidden = (v / (1.0 + jnp.exp(-v)) * up[...].astype(F32)).astype(BF16).astype(F32)
    signed = hidden * (1 - 2 * signs[...]).astype(F32)
    stacked = jnp.concatenate(
        [signed[:, p * W:(p + 1) * W] for p in range(pieces)], axis=0
    ).astype(BF16)
    right = jnp.dot(stacked, order, preferred_element_type=F32)
    parts = butterfly([right[p * Rl:(p + 1) * Rl, :] for p in range(pieces)])
    for p in range(pieces):
        for m in range(M):
            send1[m, :, p * W:(p + 1) * W] = parts[p][m * q:(m + 1) * q, :].astype(BF16)

    @pl.when(owner)
    def _():
        recv1[h] = send1[mine]

    small[3].wait()

    @pl.when(owner)
    def _():
        pl.semaphore_wait(barrier, N - 1)

    @pl.when(jnp.logical_not(owner))
    def _():
        pl.semaphore_wait(barrier, M * B + B - 1)

    def copy1(m, a):
        return pltpu.make_async_remote_copy(
            src_ref=send1.at[m], dst_ref=recv1.at[a], send_sem=s1.at[m], recv_sem=r1.at[a],
            device_id={"hid": lo + m}, device_id_type=MESH,
        )

    home = lo + lax.div(h, G)

    def copyr(g):
        return pltpu.make_async_remote_copy(
            src_ref=res, dst_ref=recvr.at[g], send_sem=sr.at[0], recv_sem=rr.at[g],
            device_id={"hid": home}, device_id_type=MESH,
        )

    but_mine(M, lo, lambda m: copy1(m, h).start())

    @pl.when(home != h)
    def _():
        copyr(lax.rem(h, G)).start()

    @pl.when(home == h)
    def _():
        recvr[lax.rem(h, G)] = res[...]

    for copy in small[4:]:
        copy.wait()
    gain[...] = gain1[...].astype(F32).reshape(1, -1)

    def copy2(t):
        peer = lax.rem(me + t, N)
        d = lax.div(peer, B)
        return pltpu.make_async_remote_copy(
            src_ref=send2.at[d], dst_ref=recv2.at[mine * B + r], send_sem=s2.at[t - 1],
            recv_sem=r2.at[mine * B + r], device_id={"hid": d, "row": lax.rem(peer, B)},
            device_id_type=MESH,
        )

    def wait2(k):
        @pl.when(lo * B + k != me)
        def _():
            pltpu.make_async_remote_copy(
                src_ref=send2.at[0], dst_ref=recv2.at[k], send_sem=s2.at[0], recv_sem=r2.at[k],
                device_id={"hid": h}, device_id_type=MESH,
            ).wait_recv()

    @pl.when(owner)
    def _():
        but_mine(A, 0, lambda a: copy1(0, a).wait_recv())
        V = min(FFl, 512)
        for c in range(0, FFl, V):
            mixed = butterfly([recv1[a, :, c:c + V].astype(F32) for a in range(A)])
            for a in range(A):
                send2[a, :, c:c + V] = (mixed[a] * (1.0 / math.sqrt(FFl * A))).astype(BF16)
        each(N, lambda t: copy2(t).start(), 1)
        recv2[mine * B + r] = send2[h]

    each(M * B, wait2)

    for j in range(J):
        wq_copy(j).start(priority=1)
    for b in range(B):
        for m in range(M):
            row = b * Rl + m * q
            lhsf[row:row + q, :] = recv2[m * B + b].astype(F32)
    lhs[...] = lhsf[...].astype(BF16)

    def copy3(m, a, j):
        return pltpu.make_async_remote_copy(
            src_ref=send3.at[j, m], dst_ref=recv3.at[j, a], send_sem=s3.at[m, j],
            recv_sem=r3.at[a, j], device_id={"hid": lo + m}, device_id_type=MESH,
        )

    def copy4(t, m, j):
        d = lax.rem(h + t, A)
        return pltpu.make_async_remote_copy(
            src_ref=send4.at[j], dst_ref=recv4.at[j, m], send_sem=s4.at[t - 1, j],
            recv_sem=r4.at[m, j], device_id={"hid": d}, device_id_type=MESH,
        )

    tile = tile_of(C, 512)

    def down_step(j):
        wd_copy(j).wait()
        for n in range(0, C, tile):
            part = jnp.dot(lhs[...], wd[j, :, n:n + tile], preferred_element_type=F32)
            for m in range(M):
                send3[j, m, :, n:n + tile] = part[m * T:(m + 1) * T, :].astype(BF16)

        but_mine(M, lo, lambda m: copy3(m, h, j).start())

        @pl.when(owner)
        def _():
            recv3[j, h] = send3[j, mine]

    loop(J, down_step)

    def stream_step(j):
        but_mine(A, 0, lambda a: copy3(0, a, j).wait_recv())
        total = recv3[j, 0].astype(F32)
        for a in range(1, A):
            total = total + recv3[j, a].astype(F32)
        columns = pl.ds(pl.multiple_of(j * C, C), C)
        total = total * (dscale[:, columns].astype(F32) * 2.0 ** (-23))
        stream = (resf[:, columns] + total).astype(BF16)
        send4[j] = stream
        recv4[j, mine] = stream
        each(A, lambda t: copy4(t, mine, j).start(), 1)

    @pl.when(owner)
    def _():
        for g in range(G):
            @pl.when(mine * G + g != h)
            def _(g=g):
                copyr(g).wait_recv()
        for g in range(G):
            resf[g * S:(g + 1) * S, :] = recvr[g].astype(F32)
        loop(J, stream_step)

    sq[...] = jnp.zeros_like(sq)
    proj[...] = jnp.zeros_like(proj)
    tile_q = tile_of(Q, 768)

    def project_step(j):
        but_mine(M, lo, lambda m: copy4(1, m, j).wait_recv())
        wq_copy(j).wait()
        for m in range(M):
            rowsf[m * T:(m + 1) * T, :] = recv4[j, m].astype(F32)
        wide = rowsf[...]
        columns = pl.ds(pl.multiple_of(j * C, C), C)
        for a in range(A):
            @pl.when(h == a)
            def _():
                ns_o[:, columns] = rowsf[a * S:(a + 1) * S, :].astype(BF16)
        lhs2[...] = (wide * gain[:, columns]).astype(BF16)
        sq[...] += jnp.sum(wide * wide, axis=1, keepdims=True)
        for n in range(0, Q, tile_q):
            proj[:, n:n + tile_q] += jnp.dot(
                lhs2[...], wq[j, :, n:n + tile_q], preferred_element_type=F32
            )

    loop(J, project_step)

    def copy5(t):
        d = lax.rem(r + t, B)
        return pltpu.make_async_remote_copy(
            src_ref=send5.at[d], dst_ref=recv5.at[r], send_sem=s5.at[t - 1],
            recv_sem=r5.at[t - 1], device_id={"row": d}, device_id_type=MESH,
        )

    for b in range(B):
        send5[b, :, :Q] = proj[b * Rl:(b + 1) * Rl, :]
        send5[b, :, Q:] = sq[b * Rl:(b + 1) * Rl, :]
    each(B, lambda t: copy5(t).start(), 1)
    recv5[r] = send5[r]

    but_mine(M, lo, lambda m: copy1(m, h).wait_send())

    @pl.when(home != h)
    def _():
        copyr(0).wait_send()

    for j in range(J):
        but_mine(M, lo, lambda m, j=j: copy3(m, h, j).wait_send())

    @pl.when(owner)
    def _():
        each(N, lambda t: copy2(t).wait_send(), 1)
        for j in range(J):
            each(A, lambda t, j=j: copy4(t, mine, j).wait_send(), 1)

    each(B, lambda t: copy5(t).wait(), 1)
    total = recv5[0]
    for b in range(1, B):
        total = total + recv5[b]
    inverse = lax.rsqrt(total[:, Q:Q + 1] / width_total + epsilon)
    out_o[...] = (
        total[:, :Q] * inverse * (qscale[...].astype(F32).reshape(1, Q) * 2.0 ** (-22))
    ).astype(BF16)


def hand_over(ns, out, ns_o, out_o, sem):
    first = pltpu.make_async_copy(ns, ns_o, sem.at[0])
    second = pltpu.make_async_copy(out, out_o, sem.at[1])
    first.start()
    second.start()
    first.wait()
    second.wait()


def body(gate, up, signs, wd, dscale, res, gain, wq, qscale):
    A = lax.axis_size("hid")
    B = lax.axis_size("row")
    N = A * B
    M = A // 2
    lo = (A - M) // 2
    Rl, FFl = gate.shape
    Dl = wd.shape[1]
    Q = wq.shape[1]
    R = Rl * B
    S = res.shape[0]
    q = Rl // M
    T = R // M
    J = 4
    C = Dl // J
    any_spec = pl.BlockSpec(memory_space=pl.ANY)
    vmem_spec = pl.BlockSpec(memory_space=pltpu.VMEM)
    dma = pltpu.SemaphoreType.DMA
    call = pl.pallas_call(
        functools.partial(kernel, A, B, J, M, lo, Dl * B),
        out_shape=(pltpu.VMEM((S, Dl), BF16), pltpu.VMEM((Rl, Q), BF16)),
        in_specs=[any_spec] * 9,
        out_specs=(vmem_spec, vmem_spec),
        scratch_shapes=[
            pltpu.VMEM((Rl, FFl), BF16),
            pltpu.VMEM((Rl, FFl), BF16),
            pltpu.VMEM((1, FFl), jnp.int32),
            pltpu.VMEM((1, Dl), jnp.int32),
            pltpu.VMEM((S, Dl), BF16),
            pltpu.VMEM((Dl,), BF16),
            pltpu.VMEM((Q,), jnp.int32),
            pltpu.VMEM((J, FFl, C), BF16),
            pltpu.VMEM((J, C, Q), BF16),
            pltpu.VMEM((1, Dl), F32),
            pltpu.VMEM((M, q, FFl), BF16),
            pltpu.VMEM((A, q, FFl), BF16),
            pltpu.VMEM((A // M, S, Dl), BF16),
            pltpu.VMEM((T, Dl), F32),
            pltpu.VMEM((A, q, FFl), BF16),
            pltpu.VMEM((M * B, q, FFl), BF16),
            pltpu.VMEM((R, FFl), F32),
            pltpu.VMEM((R, FFl), BF16),
            pltpu.VMEM((J, M, T, C), BF16),
            pltpu.VMEM((J, A, T, C), BF16),
            pltpu.VMEM((J, T, C), BF16),
            pltpu.VMEM((J, M, T, C), BF16),
            pltpu.VMEM((R, C), F32),
            pltpu.VMEM((R, C), BF16),
            pltpu.VMEM((R, 128), F32),
            pltpu.VMEM((R, Q), F32),
            pltpu.VMEM((B, Rl, Q + 128), F32),
            pltpu.VMEM((B, Rl, Q + 128), F32),
            dma((7,)),
            dma((J,)),
            dma((J,)),
            dma((M,)),
            dma((A,)),
            dma((1,)),
            dma((A // M,)),
            dma((N - 1,)),
            dma((M * B,)),
            dma((M, J)),
            dma((A, J)),
            dma((A - 1, J)),
            dma((M, J)),
            dma((B - 1,)),
            dma((B - 1,)),
        ],
        compiler_params=pltpu.CompilerParams(
            collective_id=0, has_side_effects=True, vmem_limit_bytes=62 * 1024 * 1024
        ),
    )
    made = call(
        gate, up, signs.reshape(1, -1), wd, dscale.reshape(1, -1), res, gain, wq,
        qscale,
    )
    return pl.pallas_call(
        hand_over,
        out_shape=(jax.ShapeDtypeStruct((S, Dl), BF16), jax.ShapeDtypeStruct((Rl, Q), BF16)),
        in_specs=[vmem_spec, vmem_spec],
        out_specs=(any_spec, any_spec),
        scratch_shapes=[dma((2,))],
    )(*(pltpu.with_memory_space_constraint(part, pltpu.VMEM) for part in made))


def solution(mesh):
    return jax.shard_map(
        body,
        mesh=mesh,
        in_specs=(
            P(("groups", "row"), "hid"),
            P(("groups", "row"), "hid"),
            P("hid"),
            P("hid", "row"),
            P("row"),
            P(("groups", "hid"), "row"),
            P("row"),
            P("row", "hid"),
            P("hid"),
        ),
        out_specs=(P(("groups", "hid"), "row"), P(("groups", "row"), "hid")),
        check_vma=False,
    )
```

```python
import functools
import math

import jax
import jax.numpy as jnp
from jax import lax
from jax.experimental import pallas as pl
from jax.experimental.pallas import tpu as pltpu
from jax.sharding import PartitionSpec as P

epsilon = 1e-05
F32 = jnp.float32
BF16 = jnp.bfloat16
MESH = pl.DeviceIdType.MESH


def each(count, step, start=0):
    if count - start <= 16:
        for index in range(start, count):
            step(index)
    else:

        def looped(index, carry):
            step(index)
            return carry

        lax.fori_loop(start, count, looped, 0)


def loop(count, step):
    def looped(index, carry):
        step(index)
        return carry

    lax.fori_loop(0, count, looped, 0)


def sylvester(order):
    both = lax.broadcasted_iota(jnp.int32, (order, order), 0) & lax.broadcasted_iota(
        jnp.int32, (order, order), 1
    )
    shift = 1
    while shift < order.bit_length():
        shift *= 2
    while shift > 1:
        shift //= 2
        both = both ^ lax.shift_right_logical(both, shift)
    return (1 - 2 * (both & 1)).astype(F32).astype(BF16)


def tile_of(width, largest):
    tile = largest // 128 * 128
    while width % tile:
        tile -= 128
    return tile


def butterfly(parts):
    step = 1
    while step < len(parts):
        parts = [
            parts[i] + parts[i + step] if i & step == 0 else parts[i - step] - parts[i]
            for i in range(len(parts))
        ]
        step *= 2
    return parts


def kernel(
    A, B, J, M, lo, width_total,
    gate_h, up_h, signs_h, wd_h, dscale_h, res_h, gain_h, wq_h, qscale_h,
    ns_o, out_o,
    gate, up, signs, dscale, res, gain1, qscale, wd, wq, gain,
    send1, recv1, recvr, resf, send2, recv2, lhsf, lhs, send3, recv3, send4, recv4, rowsf, lhs2,
    sq, proj, send5, recv5,
    in_sem, wd_sem, wq_sem, s1, r1, sr, rr, s2, r2, s3, r3, s4, r4, s5, r5,
):
    h = lax.axis_index("hid")
    r = lax.axis_index("row")
    N = A * B
    me = h * B + r
    mine = h - lo
    owner = (h >= lo) & (h < lo + M)
    Rl, FFl = gate.shape
    q = Rl // M
    R = Rl * B
    S = res.shape[0]
    T = R // M
    G = A // M
    C = wd.shape[2]
    Q = wq.shape[2]

    small = [
        pltpu.make_async_copy(src, dst, in_sem.at[k])
        for k, (src, dst) in enumerate(
            [(gate_h, gate), (up_h, up), (signs_h, signs), (res_h, res), (dscale_h, dscale),
             (gain_h, gain1), (qscale_h, qscale)]
        )
    ]
    barrier = pltpu.get_barrier_semaphore()

    def greet(t):
        peer = lax.rem(me + t, N)
        d = lax.div(peer, B)
        e = lax.rem(peer, B)

        @pl.when((owner & (((d >= lo) & (d < lo + M)) | (e == r))) | (d == h))
        def _():
            pl.semaphore_signal(
                barrier, inc=1, device_id={"hid": d, "row": e}, device_id_type=MESH
            )

    for copy in small[:3]:
        copy.start()
    each(N, greet, 1)
    for copy in small[3:]:
        copy.start()

    def wd_copy(j):
        return pltpu.make_async_copy(
            wd_h.at[:, pl.ds(pl.multiple_of(j * C, C), C)], wd.at[j], wd_sem.at[j]
        )

    def wq_copy(j):
        return pltpu.make_async_copy(
            wq_h.at[pl.ds(pl.multiple_of(j * C, C), C), :], wq.at[j], wq_sem.at[j]
        )

    for j in range(J):
        wd_copy(j).start(priority=1)

    def landed(part, sem):
        pltpu.make_async_copy(part, part, sem).wait()

    def all_landed(full, fewer, sem):
        @pl.when(owner)
        def _():
            landed(fewer, sem)

        @pl.when(jnp.logical_not(owner))
        def _():
            landed(full, sem)

    def but_mine(count, first, step):
        def guarded(index):
            @pl.when(first + index != h)
            def _():
                step(index)

        each(count, guarded)

    W = 256
    pieces = FFl // W
    order = sylvester(W)
    for copy in small[:3]:
        copy.wait()
    v = gate[...].astype(F32)
    hidden = (v / (1.0 + jnp.exp(-v)) * up[...].astype(F32)).astype(BF16).astype(F32)
    signed = hidden * (1 - 2 * signs[...]).astype(F32)
    stacked = jnp.concatenate(
        [signed[:, p * W:(p + 1) * W] for p in range(pieces)], axis=0
    ).astype(BF16)
    right = jnp.dot(stacked, order, preferred_element_type=F32)
    parts = butterfly([right[p * Rl:(p + 1) * Rl, :] for p in range(pieces)])
    for p in range(pieces):
        for m in range(M):
            send1[m, :, p * W:(p + 1) * W] = parts[p][m * q:(m + 1) * q, :].astype(BF16)

    @pl.when(owner)
    def _():
        recv1[h] = send1[mine]

    small[3].wait()

    @pl.when(owner)
    def _():
        pl.semaphore_wait(barrier, M * B - 1)

    @pl.when(jnp.logical_not(owner))
    def _():
        pl.semaphore_wait(barrier, M + B - 1)

    def copy1(m, a):
        return pltpu.make_async_remote_copy(
            src_ref=send1.at[m], dst_ref=recv1.at[a], send_sem=s1.at[0], recv_sem=r1.at[0],
            device_id={"hid": lo + m}, device_id_type=MESH,
        )

    home = lo + lax.div(h, G)

    def copyr(g):
        return pltpu.make_async_remote_copy(
            src_ref=res, dst_ref=recvr.at[g], send_sem=sr.at[0], recv_sem=rr.at[g],
            device_id={"hid": home}, device_id_type=MESH,
        )

    but_mine(M, lo, lambda m: copy1(m, h).start())

    @pl.when(home != h)
    def _():
        copyr(lax.rem(h, G)).start()

    @pl.when(home == h)
    def _():
        recvr[lax.rem(h, G)] = res[...]

    for copy in small[4:]:
        copy.wait()
    gain[...] = gain1[...].astype(F32).reshape(1, -1)

    def copy2(t):
        peer = lax.rem(me + t, N)
        d = lax.div(peer, B)
        e = lax.rem(peer, B)
        return pltpu.make_async_remote_copy(
            src_ref=send2.at[d], dst_ref=recv2.at[mine * B + r], send_sem=s2.at[e],
            recv_sem=r2.at[0], device_id={"hid": d, "row": e},
            device_id_type=MESH,
        )

    @pl.when(owner)
    def _():
        landed(recv1.at[pl.ds(0, A - 1)], r1.at[0])
        V = min(FFl, 512)
        for c in range(0, FFl, V):
            mixed = butterfly([recv1[a, :, c:c + V].astype(F32) for a in range(A)])
            for a in range(A):
                send2[a, :, c:c + V] = (mixed[a] * (1.0 / math.sqrt(FFl * A))).astype(BF16)
        each(N, lambda t: copy2(t).start(), 1)
        recv2[mine * B + r] = send2[h]

    all_landed(recv2, recv2.at[pl.ds(0, M * B - 1)], r2.at[0])

    for j in range(J):
        wq_copy(j).start(priority=1)
    for b in range(B):
        for m in range(M):
            row = b * Rl + m * q
            lhsf[row:row + q, :] = recv2[m * B + b].astype(F32)
    lhs[...] = lhsf[...].astype(BF16)

    def copy3(m, a, j):
        return pltpu.make_async_remote_copy(
            src_ref=send3.at[j, m], dst_ref=recv3.at[j, a], send_sem=s3.at[0],
            recv_sem=r3.at[j], device_id={"hid": lo + m}, device_id_type=MESH,
        )

    def copy4(t, m, j):
        d = lax.rem(h + t, A)
        return pltpu.make_async_remote_copy(
            src_ref=send4.at[j], dst_ref=recv4.at[j, m], send_sem=s4.at[0],
            recv_sem=r4.at[j], device_id={"hid": d}, device_id_type=MESH,
        )

    tile = tile_of(C, 512)

    def down_step(j):
        wd_copy(j).wait()
        for n in range(0, C, tile):
            part = jnp.dot(lhs[...], wd[j, :, n:n + tile], preferred_element_type=F32)
            for m in range(M):
                send3[j, m, :, n:n + tile] = part[m * T:(m + 1) * T, :].astype(BF16)

        but_mine(M, lo, lambda m: copy3(m, h, j).start())

        @pl.when(owner)
        def _():
            recv3[j, h] = send3[j, mine]

    loop(J, down_step)

    def stream_step(j):
        landed(recv3.at[j, pl.ds(0, A - 1)], r3.at[j])
        total = recv3[j, 0].astype(F32)
        for a in range(1, A):
            total = total + recv3[j, a].astype(F32)
        columns = pl.ds(pl.multiple_of(j * C, C), C)
        total = total * (dscale[:, columns].astype(F32) * 2.0 ** (-23))
        stream = (resf[:, columns] + total).astype(BF16)
        send4[j] = stream
        recv4[j, mine] = stream
        each(A, lambda t: copy4(t, mine, j).start(), 1)

    @pl.when(owner)
    def _():
        for g in range(G):
            @pl.when(mine * G + g != h)
            def _(g=g):
                copyr(g).wait_recv()
        for g in range(G):
            resf[g * S:(g + 1) * S, :] = recvr[g].astype(F32)
        loop(J, stream_step)

    sq[...] = jnp.zeros_like(sq)
    proj[...] = jnp.zeros_like(proj)
    tile_q = tile_of(Q, 768)

    def project_step(j):
        all_landed(recv4.at[j], recv4.at[j, pl.ds(0, M - 1)], r4.at[j])
        wq_copy(j).wait()
        for m in range(M):
            rowsf[m * T:(m + 1) * T, :] = recv4[j, m].astype(F32)
        wide = rowsf[...]
        columns = pl.ds(pl.multiple_of(j * C, C), C)
        for a in range(A):
            @pl.when(h == a)
            def _():
                ns_o[:, columns] = rowsf[a * S:(a + 1) * S, :].astype(BF16)
        lhs2[...] = (wide * gain[:, columns]).astype(BF16)
        sq[...] += jnp.sum(wide * wide, axis=1, keepdims=True)
        for n in range(0, Q, tile_q):
            proj[:, n:n + tile_q] += jnp.dot(
                lhs2[...], wq[j, :, n:n + tile_q], preferred_element_type=F32
            )

    loop(J, project_step)

    def copy5(t):
        d = lax.rem(r + t, B)
        return pltpu.make_async_remote_copy(
            src_ref=send5.at[d], dst_ref=recv5.at[r], send_sem=s5.at[t - 1],
            recv_sem=r5.at[t - 1], device_id={"row": d}, device_id_type=MESH,
        )

    for b in range(B):
        send5[b, :, :Q] = proj[b * Rl:(b + 1) * Rl, :]
        send5[b, :, Q:] = sq[b * Rl:(b + 1) * Rl, :]
    each(B, lambda t: copy5(t).start(), 1)
    recv5[r] = send5[r]

    all_landed(send1, send1.at[pl.ds(0, M - 1)], s1.at[0])
    all_landed(send3, send3.at[:, pl.ds(0, M - 1)], s3.at[0])

    @pl.when(home != h)
    def _():
        copyr(0).wait_send()

    @pl.when(owner)
    def _():
        landed(recv3.at[:, pl.ds(0, A - 1)], s4.at[0])
        for e in range(B):
            @pl.when(r == e)
            def _(e=e):
                landed(send2.at[pl.ds(0, A - 1)], s2.at[e])

            @pl.when(r != e)
            def _(e=e):
                landed(send2, s2.at[e])

    each(B, lambda t: copy5(t).wait(), 1)
    total = recv5[0]
    for b in range(1, B):
        total = total + recv5[b]
    inverse = lax.rsqrt(total[:, Q:Q + 1] / width_total + epsilon)
    out_o[...] = (
        total[:, :Q] * inverse * (qscale[...].astype(F32).reshape(1, Q) * 2.0 ** (-22))
    ).astype(BF16)


def hand_over(ns, out, ns_o, out_o, sem):
    first = pltpu.make_async_copy(ns, ns_o, sem.at[0])
    second = pltpu.make_async_copy(out, out_o, sem.at[1])
    first.start()
    second.start()
    first.wait()
    second.wait()


def body(gate, up, signs, wd, dscale, res, gain, wq, qscale):
    A = lax.axis_size("hid")
    B = lax.axis_size("row")
    N = A * B
    M = A // 2
    lo = (A - M) // 2
    Rl, FFl = gate.shape
    Dl = wd.shape[1]
    Q = wq.shape[1]
    R = Rl * B
    S = res.shape[0]
    q = Rl // M
    T = R // M
    J = 8 if Dl % (8 * 128) == 0 else 4
    C = Dl // J
    any_spec = pl.BlockSpec(memory_space=pl.ANY)
    vmem_spec = pl.BlockSpec(memory_space=pltpu.VMEM)
    dma = pltpu.SemaphoreType.DMA
    call = pl.pallas_call(
        functools.partial(kernel, A, B, J, M, lo, Dl * B),
        out_shape=(pltpu.VMEM((S, Dl), BF16), pltpu.VMEM((Rl, Q), BF16)),
        in_specs=[any_spec] * 9,
        out_specs=(vmem_spec, vmem_spec),
        scratch_shapes=[
            pltpu.VMEM((Rl, FFl), BF16),
            pltpu.VMEM((Rl, FFl), BF16),
            pltpu.VMEM((1, FFl), jnp.int32),
            pltpu.VMEM((1, Dl), jnp.int32),
            pltpu.VMEM((S, Dl), BF16),
            pltpu.VMEM((Dl,), BF16),
            pltpu.VMEM((Q,), jnp.int32),
            pltpu.VMEM((J, FFl, C), BF16),
            pltpu.VMEM((J, C, Q), BF16),
            pltpu.VMEM((1, Dl), F32),
            pltpu.VMEM((M, q, FFl), BF16),
            pltpu.VMEM((A, q, FFl), BF16),
            pltpu.VMEM((A // M, S, Dl), BF16),
            pltpu.VMEM((T, Dl), F32),
            pltpu.VMEM((A, q, FFl), BF16),
            pltpu.VMEM((M * B, q, FFl), BF16),
            pltpu.VMEM((R, FFl), F32),
            pltpu.VMEM((R, FFl), BF16),
            pltpu.VMEM((J, M, T, C), BF16),
            pltpu.VMEM((J, A, T, C), BF16),
            pltpu.VMEM((J, T, C), BF16),
            pltpu.VMEM((J, M, T, C), BF16),
            pltpu.VMEM((R, C), F32),
            pltpu.VMEM((R, C), BF16),
            pltpu.VMEM((R, 128), F32),
            pltpu.VMEM((R, Q), F32),
            pltpu.VMEM((B, Rl, Q + 128), F32),
            pltpu.VMEM((B, Rl, Q + 128), F32),
            dma((7,)),
            dma((J,)),
            dma((J,)),
            dma((1,)),
            dma((1,)),
            dma((1,)),
            dma((A // M,)),
            dma((B,)),
            dma((1,)),
            dma((1,)),
            dma((J,)),
            dma((1,)),
            dma((J,)),
            dma((B - 1,)),
            dma((B - 1,)),
        ],
        compiler_params=pltpu.CompilerParams(
            collective_id=0, has_side_effects=True, vmem_limit_bytes=62 * 1024 * 1024
        ),
    )
    made = call(
        gate, up, signs.reshape(1, -1), wd, dscale.reshape(1, -1), res, gain, wq,
        qscale,
    )
    return pl.pallas_call(
        hand_over,
        out_shape=(jax.ShapeDtypeStruct((S, Dl), BF16), jax.ShapeDtypeStruct((Rl, Q), BF16)),
        in_specs=[vmem_spec, vmem_spec],
        out_specs=(any_spec, any_spec),
        scratch_shapes=[dma((2,))],
    )(*(pltpu.with_memory_space_constraint(part, pltpu.VMEM) for part in made))


def solution(mesh):
    return jax.shard_map(
        body,
        mesh=mesh,
        in_specs=(
            P(("groups", "row"), "hid"),
            P(("groups", "row"), "hid"),
            P("hid"),
            P("hid", "row"),
            P("row"),
            P(("groups", "hid"), "row"),
            P("row"),
            P("row", "hid"),
            P("hid"),
        ),
        out_specs=(P(("groups", "hid"), "row"), P(("groups", "row"), "hid")),
        check_vma=False,
    )
```

```python
import functools
import math

import jax
import jax.numpy as jnp
from jax import lax
from jax.experimental import pallas as pl
from jax.experimental.pallas import tpu as pltpu
from jax.sharding import PartitionSpec as P

epsilon = 1e-05
F32 = jnp.float32
BF16 = jnp.bfloat16
MESH = pl.DeviceIdType.MESH


def each(count, step, start=0):
    if count - start <= 16:
        for index in range(start, count):
            step(index)
    else:

        def looped(index, carry):
            step(index)
            return carry

        lax.fori_loop(start, count, looped, 0)


def loop(count, step, start=0):
    def looped(index, carry):
        step(index)
        return carry

    lax.fori_loop(start, count, looped, 0)


def sylvester(order):
    both = lax.broadcasted_iota(jnp.int32, (order, order), 0) & lax.broadcasted_iota(
        jnp.int32, (order, order), 1
    )
    shift = 1
    while shift < order.bit_length():
        shift *= 2
    while shift > 1:
        shift //= 2
        both = both ^ lax.shift_right_logical(both, shift)
    return (1 - 2 * (both & 1)).astype(F32).astype(BF16)


def tile_of(width, largest):
    tile = largest // 128 * 128
    while width % tile:
        tile -= 128
    return tile


def butterfly(parts):
    step = 1
    while step < len(parts):
        parts = [
            parts[i] + parts[i + step] if i & step == 0 else parts[i - step] - parts[i]
            for i in range(len(parts))
        ]
        step *= 2
    return parts


def kernel(
    A, B, J, KC, E, M, lo, width_total,
    gate_h, up_h, signs_h, wd_h, dscale_h, res_h, gain_h, wq_h, qscale_h,
    ns_o, out_o,
    gate, up, signs, dscale, res, gain1, qscale, wd, wq, gain,
    send1, recv1, recvr, resf, send2, recv2, lhsf, lhs, send3, recv3, send4, recv4, rowsf, lhs2,
    sq, proj, early, send5, recv5,
    in_sem, wd_sem, wq_sem, s1, r1, sr, rr, s2, r2, s3, r3, s4, r4, s5, r5,
):
    h = lax.axis_index("hid")
    r = lax.axis_index("row")
    N = A * B
    me = h * B + r
    mine = h - lo
    owner = (h >= lo) & (h < lo + M)
    Rl, FFl = gate.shape
    q = Rl // M
    R = Rl * B
    S = res.shape[0]
    T = R // M
    G = A // M
    C = wd.shape[2]
    Q = wq.shape[2]

    small = [
        pltpu.make_async_copy(src, dst, in_sem.at[k])
        for k, (src, dst) in enumerate(
            [(gate_h, gate), (up_h, up), (signs_h, signs), (res_h, res), (dscale_h, dscale),
             (gain_h, gain1), (qscale_h, qscale)]
        )
    ]
    barrier = pltpu.get_barrier_semaphore()

    def greet(t):
        peer = lax.rem(me + t, N)
        d = lax.div(peer, B)
        e = lax.rem(peer, B)

        @pl.when((owner & (((d >= lo) & (d < lo + M)) | (e == r))) | (d == h))
        def _():
            pl.semaphore_signal(
                barrier, inc=1, device_id={"hid": d, "row": e}, device_id_type=MESH
            )

    for copy in small[:3]:
        copy.start()
    each(N, greet, 1)
    for copy in small[3:]:
        copy.start()

    def wd_copy(j):
        return pltpu.make_async_copy(
            wd_h.at[:, pl.ds(pl.multiple_of(j * C, C), C)], wd.at[j], wd_sem.at[j]
        )

    def wq_copy(j):
        return pltpu.make_async_copy(
            wq_h.at[pl.ds(pl.multiple_of(j * C, C), C), :], wq.at[j], wq_sem.at[j]
        )

    for j in range(J):
        wd_copy(j).start(priority=1)

    def landed(part, sem):
        pltpu.make_async_copy(part, part, sem).wait()

    def all_landed(full, fewer, sem):
        @pl.when(owner)
        def _():
            landed(fewer, sem)

        @pl.when(jnp.logical_not(owner))
        def _():
            landed(full, sem)

    L = FFl // KC

    def but_mine(count, first, step):
        def guarded(index):
            @pl.when(first + index != h)
            def _():
                step(index)

        each(count, guarded)

    W = 256
    pieces = FFl // W
    order = sylvester(W)
    for copy in small[:3]:
        copy.wait()
    v = gate[...].astype(F32)
    hidden = (v / (1.0 + jnp.exp(-v)) * up[...].astype(F32)).astype(BF16).astype(F32)
    signed = hidden * (1 - 2 * signs[...]).astype(F32)
    stacked = jnp.concatenate(
        [signed[:, p * W:(p + 1) * W] for p in range(pieces)], axis=0
    ).astype(BF16)
    right = jnp.dot(stacked, order, preferred_element_type=F32)
    parts = butterfly([right[p * Rl:(p + 1) * Rl, :] for p in range(pieces)])
    for p in range(pieces):
        c, w = p * W // L, p * W % L
        for m in range(M):
            send1[c, m, :, w:w + W] = parts[p][m * q:(m + 1) * q, :].astype(BF16)

    @pl.when(owner)
    def _():
        for c in range(KC):
            recv1[c, h] = send1[c, mine]

    small[3].wait()

    @pl.when(owner)
    def _():
        pl.semaphore_wait(barrier, M * B - 1)

    @pl.when(jnp.logical_not(owner))
    def _():
        pl.semaphore_wait(barrier, M + B - 1)

    def copy1(c, m, a):
        return pltpu.make_async_remote_copy(
            src_ref=send1.at[c, m], dst_ref=recv1.at[c, a], send_sem=s1.at[0], recv_sem=r1.at[c],
            device_id={"hid": lo + m}, device_id_type=MESH,
        )

    home = lo + lax.div(h, G)

    def copyr(g):
        return pltpu.make_async_remote_copy(
            src_ref=res, dst_ref=recvr.at[g], send_sem=sr.at[0], recv_sem=rr.at[g],
            device_id={"hid": home}, device_id_type=MESH,
        )

    late = lax.div(h, (A + 1) // 2)

    def far_first(step):
        def guarded(index):
            m = late * index + (1 - late) * (M - 1 - index)

            @pl.when(lo + m != h)
            def _():
                step(m)

        each(M, guarded)

    for c in range(KC):
        far_first(lambda m, c=c: copy1(c, m, h).start())

    @pl.when(home != h)
    def _():
        copyr(lax.rem(h, G)).start()

    @pl.when(home == h)
    def _():
        recvr[lax.rem(h, G)] = res[...]

    for copy in small[4:]:
        copy.wait()
    gain[...] = gain1[...].astype(F32).reshape(1, -1)

    def copy2(c, t):
        peer = lax.rem(me + t, N)
        d = lax.div(peer, B)
        e = lax.rem(peer, B)
        return pltpu.make_async_remote_copy(
            src_ref=send2.at[c, d], dst_ref=recv2.at[c, mine * B + r], send_sem=s2.at[e],
            recv_sem=r2.at[c], device_id={"hid": d, "row": e},
            device_id_type=MESH,
        )

    @pl.when(owner)
    def _():
        V = min(L, 512)
        for c in range(KC):
            landed(recv1.at[c, pl.ds(0, A - 1)], r1.at[c])
            for n in range(0, L, V):
                mixed = butterfly([recv1[c, a, :, n:n + V].astype(F32) for a in range(A)])
                for a in range(A):
                    send2[c, a, :, n:n + V] = (mixed[a] * (1.0 / math.sqrt(FFl * A))).astype(BF16)
            each(N, lambda t, c=c: copy2(c, t).start(), 1)
            recv2[c, mine * B + r] = send2[c, h]

    for j in range(J):
        wq_copy(j).start(priority=1)
    def gather(c):
        all_landed(recv2.at[c], recv2.at[c, pl.ds(0, M * B - 1)], r2.at[c])
        for b in range(B):
            for m in range(M):
                row = b * Rl + m * q
                lhsf[row:row + q, :] = recv2[c, m * B + b].astype(F32)
        lhs[:, c * L:(c + 1) * L] = lhsf[...].astype(BF16)

    def copy3(m, a, j):
        return pltpu.make_async_remote_copy(
            src_ref=send3.at[j, m], dst_ref=recv3.at[j, a], send_sem=s3.at[0],
            recv_sem=r3.at[j], device_id={"hid": lo + m}, device_id_type=MESH,
        )

    def copy4(t, m, j):
        d = lax.rem(h + t, A)
        return pltpu.make_async_remote_copy(
            src_ref=send4.at[j], dst_ref=recv4.at[j, m], send_sem=s4.at[0],
            recv_sem=r4.at[j], device_id={"hid": d}, device_id_type=MESH,
        )

    tile = tile_of(C, 512)

    def product(j, n, c, count):
        return jnp.dot(
            lhs[:, c * L:(c + count) * L], wd[j, c * L:(c + count) * L, n:n + tile],
            preferred_element_type=F32,
        )

    def send_sums(j):
        far_first(lambda m: copy3(m, h, j).start())

        @pl.when(owner)
        def _():
            recv3[j, h] = send3[j, mine]

    def put(j, n, part):
        for m in range(M):
            send3[j, m, :, n:n + tile] = part[m * T:(m + 1) * T, :].astype(BF16)

    def first_step(j):
        wd_copy(j).wait()
        for n in range(0, C, tile):
            early[j, :, n:n + tile] = product(j, n, 0, 1)

    def second_step(j):
        for n in range(0, C, tile):
            put(j, n, early[j, :, n:n + tile] + product(j, n, 1, KC - 1))
        send_sums(j)

    def down_step(j):
        wd_copy(j).wait()
        for n in range(0, C, tile):
            put(j, n, product(j, n, 0, KC))
        send_sums(j)

    gather(0)
    loop(E, first_step)
    gather(1)
    loop(E, second_step)
    loop(J, down_step, E)

    def stream_step(j):
        landed(recv3.at[j, pl.ds(0, A - 1)], r3.at[j])
        total = recv3[j, 0].astype(F32)
        for a in range(1, A):
            total = total + recv3[j, a].astype(F32)
        columns = pl.ds(pl.multiple_of(j * C, C), C)
        total = total * (dscale[:, columns].astype(F32) * 2.0 ** (-23))
        stream = (resf[:, columns] + total).astype(BF16)
        send4[j] = stream
        recv4[j, mine] = stream
        each(A, lambda t: copy4(t, mine, j).start(), 1)

    @pl.when(owner)
    def _():
        for g in range(G):
            @pl.when(mine * G + g != h)
            def _(g=g):
                copyr(g).wait_recv()
        for g in range(G):
            resf[g * S:(g + 1) * S, :] = recvr[g].astype(F32)
        loop(J, stream_step)

    sq[...] = jnp.zeros_like(sq)
    proj[...] = jnp.zeros_like(proj)
    tile_q = tile_of(Q, 768)

    def project_step(j):
        all_landed(recv4.at[j], recv4.at[j, pl.ds(0, M - 1)], r4.at[j])
        wq_copy(j).wait()
        for m in range(M):
            rowsf[m * T:(m + 1) * T, :] = recv4[j, m].astype(F32)
        wide = rowsf[...]
        columns = pl.ds(pl.multiple_of(j * C, C), C)
        for a in range(A):
            @pl.when(h == a)
            def _():
                ns_o[:, columns] = rowsf[a * S:(a + 1) * S, :].astype(BF16)
        lhs2[...] = (wide * gain[:, columns]).astype(BF16)
        sq[...] += jnp.sum(wide * wide, axis=1, keepdims=True)
        for n in range(0, Q, tile_q):
            proj[:, n:n + tile_q] += jnp.dot(
                lhs2[...], wq[j, :, n:n + tile_q], preferred_element_type=F32
            )

    loop(J, project_step)

    def copy5(t):
        d = lax.rem(r + t, B)
        return pltpu.make_async_remote_copy(
            src_ref=send5.at[d], dst_ref=recv5.at[r], send_sem=s5.at[t - 1],
            recv_sem=r5.at[t - 1], device_id={"row": d}, device_id_type=MESH,
        )

    for b in range(B):
        send5[b, :, :Q] = proj[b * Rl:(b + 1) * Rl, :]
        send5[b, :, Q:] = sq[b * Rl:(b + 1) * Rl, :]
    each(B, lambda t: copy5(t).start(), 1)
    recv5[r] = send5[r]

    all_landed(send1, send1.at[:, pl.ds(0, M - 1)], s1.at[0])
    all_landed(send3, send3.at[:, pl.ds(0, M - 1)], s3.at[0])

    @pl.when(home != h)
    def _():
        copyr(0).wait_send()

    @pl.when(owner)
    def _():
        landed(recv3.at[:, pl.ds(0, A - 1)], s4.at[0])
        for e in range(B):
            @pl.when(r == e)
            def _(e=e):
                landed(send2.at[:, pl.ds(0, A - 1)], s2.at[e])

            @pl.when(r != e)
            def _(e=e):
                landed(send2, s2.at[e])

    each(B, lambda t: copy5(t).wait(), 1)
    total = recv5[0]
    for b in range(1, B):
        total = total + recv5[b]
    inverse = lax.rsqrt(total[:, Q:Q + 1] / width_total + epsilon)
    out_o[...] = (
        total[:, :Q] * inverse * (qscale[...].astype(F32).reshape(1, Q) * 2.0 ** (-22))
    ).astype(BF16)


def hand_over(ns, out, ns_o, out_o, sem):
    first = pltpu.make_async_copy(ns, ns_o, sem.at[0])
    second = pltpu.make_async_copy(out, out_o, sem.at[1])
    first.start()
    second.start()
    first.wait()
    second.wait()


def body(gate, up, signs, wd, dscale, res, gain, wq, qscale):
    A = lax.axis_size("hid")
    B = lax.axis_size("row")
    N = A * B
    M = A // 2
    lo = (A - M) // 2
    Rl, FFl = gate.shape
    Dl = wd.shape[1]
    Q = wq.shape[1]
    R = Rl * B
    S = res.shape[0]
    q = Rl // M
    T = R // M
    J = 4 if Dl % (4 * 128) == 0 else 4
    C = Dl // J
    KC = 2
    E = 1
    L = FFl // KC
    any_spec = pl.BlockSpec(memory_space=pl.ANY)
    vmem_spec = pl.BlockSpec(memory_space=pltpu.VMEM)
    dma = pltpu.SemaphoreType.DMA
    call = pl.pallas_call(
        functools.partial(kernel, A, B, J, KC, E, M, lo, Dl * B),
        out_shape=(pltpu.VMEM((S, Dl), BF16), pltpu.VMEM((Rl, Q), BF16)),
        in_specs=[any_spec] * 9,
        out_specs=(vmem_spec, vmem_spec),
        scratch_shapes=[
            pltpu.VMEM((Rl, FFl), BF16),
            pltpu.VMEM((Rl, FFl), BF16),
            pltpu.VMEM((1, FFl), jnp.int32),
            pltpu.VMEM((1, Dl), jnp.int32),
            pltpu.VMEM((S, Dl), BF16),
            pltpu.VMEM((Dl,), BF16),
            pltpu.VMEM((Q,), jnp.int32),
            pltpu.VMEM((J, FFl, C), BF16),
            pltpu.VMEM((J, C, Q), BF16),
            pltpu.VMEM((1, Dl), F32),
            pltpu.VMEM((KC, M, q, L), BF16),
            pltpu.VMEM((KC, A, q, L), BF16),
            pltpu.VMEM((A // M, S, Dl), BF16),
            pltpu.VMEM((T, Dl), F32),
            pltpu.VMEM((KC, A, q, L), BF16),
            pltpu.VMEM((KC, M * B, q, L), BF16),
            pltpu.VMEM((R, L), F32),
            pltpu.VMEM((R, FFl), BF16),
            pltpu.VMEM((J, M, T, C), BF16),
            pltpu.VMEM((J, A, T, C), BF16),
            pltpu.VMEM((J, T, C), BF16),
            pltpu.VMEM((J, M, T, C), BF16),
            pltpu.VMEM((R, C), F32),
            pltpu.VMEM((R, C), BF16),
            pltpu.VMEM((R, 128), F32),
            pltpu.VMEM((R, Q), F32),
            pltpu.VMEM((E, R, C), F32),
            pltpu.VMEM((B, Rl, Q + 128), F32),
            pltpu.VMEM((B, Rl, Q + 128), F32),
            dma((7,)),
            dma((J,)),
            dma((J,)),
            dma((1,)),
            dma((KC,)),
            dma((1,)),
            dma((A // M,)),
            dma((B,)),
            dma((KC,)),
            dma((1,)),
            dma((J,)),
            dma((1,)),
            dma((J,)),
            dma((B - 1,)),
            dma((B - 1,)),
        ],
        compiler_params=pltpu.CompilerParams(
            collective_id=0, has_side_effects=True, vmem_limit_bytes=62 * 1024 * 1024
        ),
    )
    made = call(
        gate, up, signs.reshape(1, -1), wd, dscale.reshape(1, -1), res, gain, wq,
        qscale,
    )
    return pl.pallas_call(
        hand_over,
        out_shape=(jax.ShapeDtypeStruct((S, Dl), BF16), jax.ShapeDtypeStruct((Rl, Q), BF16)),
        in_specs=[vmem_spec, vmem_spec],
        out_specs=(any_spec, any_spec),
        scratch_shapes=[dma((2,))],
    )(*(pltpu.with_memory_space_constraint(part, pltpu.VMEM) for part in made))


def solution(mesh):
    return jax.shard_map(
        body,
        mesh=mesh,
        in_specs=(
            P(("groups", "row"), "hid"),
            P(("groups", "row"), "hid"),
            P("hid"),
            P("hid", "row"),
            P("row"),
            P(("groups", "hid"), "row"),
            P("row"),
            P("row", "hid"),
            P("hid"),
        ),
        out_specs=(P(("groups", "hid"), "row"), P(("groups", "row"), "hid")),
        check_vma=False,
    )
```

```python
import functools
import math

import jax
import jax.numpy as jnp
from jax import lax
from jax.experimental import pallas as pl
from jax.experimental.pallas import tpu as pltpu
from jax.sharding import PartitionSpec as P

epsilon = 1e-05
F32 = jnp.float32
BF16 = jnp.bfloat16
MESH = pl.DeviceIdType.MESH


def each(count, step, start=0):
    if count - start <= 16:
        for index in range(start, count):
            step(index)
    else:

        def looped(index, carry):
            step(index)
            return carry

        lax.fori_loop(start, count, looped, 0)


def loop(count, step, start=0):
    def looped(index, carry):
        step(index)
        return carry

    lax.fori_loop(start, count, looped, 0)


def sylvester(order):
    both = lax.broadcasted_iota(jnp.int32, (order, order), 0) & lax.broadcasted_iota(
        jnp.int32, (order, order), 1
    )
    shift = 1
    while shift < order.bit_length():
        shift *= 2
    while shift > 1:
        shift //= 2
        both = both ^ lax.shift_right_logical(both, shift)
    return (1 - 2 * (both & 1)).astype(F32).astype(BF16)


def tile_of(width, largest):
    tile = largest // 128 * 128
    while width % tile:
        tile -= 128
    return tile


def butterfly(parts):
    step = 1
    while step < len(parts):
        parts = [
            parts[i] + parts[i + step] if i & step == 0 else parts[i - step] - parts[i]
            for i in range(len(parts))
        ]
        step *= 2
    return parts


def kernel(
    A, B, J, KC, pairs, M, lo, width_total,
    gate_h, up_h, signs_h, wd_h, dscale_h, res_h, gain_h, wq_h, qscale_h,
    ns_o, out_o,
    gate, up, signs, dscale, res, gain1, qscale, wd, wq, gain,
    send1, recv1, recvr, resf, send2, recv2, lhsf, lhs, send3, recv3, send4, recv4, rowsf, lhs2,
    sq, proj, early, send5, recv5,
    in_sem, wd_sem, wq_sem, s1, r1, sr, rr, s2, r2, s3, r3, s4, r4, s5, r5,
):
    h = lax.axis_index("hid")
    r = lax.axis_index("row")
    N = A * B
    me = h * B + r
    mine = h - lo
    owner = (h >= lo) & (h < lo + M)
    Rl, FFl = gate.shape
    q = Rl // M
    R = Rl * B
    S = res.shape[0]
    T = R // M
    G = A // M
    C = wd.shape[2]
    Q = wq.shape[1]

    small = [
        pltpu.make_async_copy(src, dst, in_sem.at[k])
        for k, (src, dst) in enumerate(
            [(gate_h, gate), (up_h, up), (signs_h, signs), (res_h, res), (dscale_h, dscale),
             (gain_h, gain1), (qscale_h, qscale)]
        )
    ]
    barrier = pltpu.get_barrier_semaphore()

    def greet(t):
        peer = lax.rem(me + t, N)
        d = lax.div(peer, B)
        e = lax.rem(peer, B)

        @pl.when((owner & (((d >= lo) & (d < lo + M)) | (e == r))) | (d == h))
        def _():
            pl.semaphore_signal(
                barrier, inc=1, device_id={"hid": d, "row": e}, device_id_type=MESH
            )

    for copy in small[:3]:
        copy.start()
    each(N, greet, 1)
    for copy in small[3:]:
        copy.start()

    def wd_copy(j):
        return pltpu.make_async_copy(
            wd_h.at[:, pl.ds(pl.multiple_of(j * C, C), C)], wd.at[j], wd_sem.at[j]
        )

    def wq_copy(j):
        return pltpu.make_async_copy(
            wq_h.at[pl.ds(pl.multiple_of(j * C, C), C), :], wq.at[pl.ds(pl.multiple_of(j * C, C), C), :], wq_sem.at[j]
        )

    for j in range(J):
        wd_copy(j).start(priority=1)

    def landed(part, sem):
        pltpu.make_async_copy(part, part, sem).wait()

    def all_landed(full, fewer, sem):
        @pl.when(owner)
        def _():
            landed(fewer, sem)

        @pl.when(jnp.logical_not(owner))
        def _():
            landed(full, sem)

    L = FFl // KC

    def but_mine(count, first, step):
        def guarded(index):
            @pl.when(first + index != h)
            def _():
                step(index)

        each(count, guarded)

    W = 256
    pieces = FFl // W
    order = sylvester(W)
    for copy in small[:3]:
        copy.wait()
    v = gate[...].astype(F32)
    hidden = (v / (1.0 + jnp.exp(-v)) * up[...].astype(F32)).astype(BF16).astype(F32)
    signed = hidden * (1 - 2 * signs[...]).astype(F32)
    stacked = jnp.concatenate(
        [signed[:, p * W:(p + 1) * W] for p in range(pieces)], axis=0
    ).astype(BF16)
    right = jnp.dot(stacked, order, preferred_element_type=F32)
    parts = butterfly([right[p * Rl:(p + 1) * Rl, :] for p in range(pieces)])
    for p in range(pieces):
        c, w = p * W // L, p * W % L
        for m in range(M):
            send1[c, m, :, w:w + W] = parts[p][m * q:(m + 1) * q, :].astype(BF16)

    @pl.when(owner)
    def _():
        for c in range(KC):
            recv1[c, h] = send1[c, mine]

    small[3].wait()

    @pl.when(owner)
    def _():
        pl.semaphore_wait(barrier, M * B - 1)

    @pl.when(jnp.logical_not(owner))
    def _():
        pl.semaphore_wait(barrier, M + B - 1)

    def copy1(c, m, a):
        return pltpu.make_async_remote_copy(
            src_ref=send1.at[c, m], dst_ref=recv1.at[c, a], send_sem=s1.at[0], recv_sem=r1.at[c],
            device_id={"hid": lo + m}, device_id_type=MESH,
        )

    home = lo + lax.div(h, G)

    def copyr(g):
        return pltpu.make_async_remote_copy(
            src_ref=res, dst_ref=recvr.at[g], send_sem=sr.at[0], recv_sem=rr.at[g],
            device_id={"hid": home}, device_id_type=MESH,
        )

    late = lax.div(h, (A + 1) // 2)

    def far_first(step):
        def guarded(index):
            m = late * index + (1 - late) * (M - 1 - index)

            @pl.when(lo + m != h)
            def _():
                step(m)

        each(M, guarded)

    for c in range(KC):
        far_first(lambda m, c=c: copy1(c, m, h).start())

    @pl.when(home != h)
    def _():
        copyr(lax.rem(h, G)).start()

    @pl.when(home == h)
    def _():
        recvr[lax.rem(h, G)] = res[...]

    for copy in small[4:]:
        copy.wait()
    gain[...] = gain1[...].astype(F32).reshape(1, -1)

    def far(index, count):
        return late * index + (1 - late) * (count - 1 - index)

    def copy2(c, t):
        peer = far(t, N)
        d = lax.div(peer, B)
        e = lax.rem(peer, B)
        return pltpu.make_async_remote_copy(
            src_ref=send2.at[c, d], dst_ref=recv2.at[c, mine * B + r], send_sem=s2.at[e],
            recv_sem=r2.at[c], device_id={"hid": d, "row": e},
            device_id_type=MESH,
        )

    @pl.when(owner)
    def _():
        V = min(L, 512)
        for c in range(KC):
            landed(recv1.at[c, pl.ds(0, A - 1)], r1.at[c])
            for n in range(0, L, V):
                mixed = butterfly([recv1[c, a, :, n:n + V].astype(F32) for a in range(A)])
                for a in range(A):
                    send2[c, a, :, n:n + V] = (mixed[a] * (1.0 / math.sqrt(FFl * A))).astype(BF16)

            def send_rotated(t, c=c):
                @pl.when(far(t, N) != me)
                def _():
                    copy2(c, t).start()

            each(N, send_rotated)
            recv2[c, mine * B + r] = send2[c, h]

    for j in range(J):
        wq_copy(j).start(priority=1)
    def gather(c):
        all_landed(recv2.at[c], recv2.at[c, pl.ds(0, M * B - 1)], r2.at[c])
        for b in range(B):
            for m in range(M):
                row = b * Rl + m * q
                lhsf[row:row + q, :] = recv2[c, m * B + b].astype(F32)
        lhs[:, c * L:(c + 1) * L] = lhsf[...].astype(BF16)

    def copy3(m, a, unit, width, g):
        return pltpu.make_async_remote_copy(
            src_ref=send3.at[m, pl.ds(unit, width)], dst_ref=recv3.at[a, pl.ds(unit, width)],
            send_sem=s3.at[0], recv_sem=r3.at[g], device_id={"hid": lo + m}, device_id_type=MESH,
        )

    def copy4(t, m, unit, width, g):
        d = far(t, A)
        return pltpu.make_async_remote_copy(
            src_ref=send4.at[pl.ds(unit, width)], dst_ref=recv4.at[m, pl.ds(unit, width)],
            send_sem=s4.at[0], recv_sem=r4.at[g], device_id={"hid": d}, device_id_type=MESH,
        )

    def groups(step, start=0):
        loop(pairs, lambda g: step(2 * g, 2, g), start)
        loop(pairs + 2, lambda g: step(pairs + g, 1, g), pairs)

    tile = tile_of(C, 512)

    def product(j, n, c, count):
        return jnp.dot(
            lhs[:, c * L:(c + count) * L], wd[j, c * L:(c + count) * L, n:n + tile],
            preferred_element_type=F32,
        )

    def send_sums(unit, width, g):
        far_first(lambda m: copy3(m, h, unit, width, g).start())

        @pl.when(owner)
        def _():
            recv3[h, pl.ds(unit, width)] = send3[mine, pl.ds(unit, width)]

    def put(j, n, part):
        for m in range(M):
            send3[m, j, :, n:n + tile] = part[m * T:(m + 1) * T, :].astype(BF16)

    def first_step():
        for j in range(2):
            wd_copy(j).wait()
            for n in range(0, C, tile):
                early[j, :, n:n + tile] = product(j, n, 0, 1)

    def second_step():
        for j in range(2):
            for n in range(0, C, tile):
                put(j, n, early[j, :, n:n + tile] + product(j, n, 1, KC - 1))
        send_sums(0, 2, 0)

    def down_step(unit, width, g):
        for u in range(width):
            wd_copy(unit + u).wait()
        for u in range(width):
            for n in range(0, C, tile):
                put(unit + u, n, product(unit + u, n, 0, KC))
        send_sums(unit, width, g)

    gather(0)
    first_step()
    gather(1)
    second_step()
    groups(down_step, 1)

    def stream_step(unit, width, g):
        landed(recv3.at[pl.ds(0, A - 1), pl.ds(unit, width)], r3.at[g])
        for u in range(width):
            j = unit + u
            total = recv3[0, j].astype(F32)
            for a in range(1, A):
                total = total + recv3[a, j].astype(F32)
            columns = pl.ds(pl.multiple_of(j * C, C), C)
            total = total * (dscale[:, columns].astype(F32) * 2.0 ** (-23))
            stream = (resf[:, columns] + total).astype(BF16)
            send4[j] = stream
            recv4[mine, j] = stream

        def send_stream(t):
            @pl.when(far(t, A) != h)
            def _():
                copy4(t, mine, unit, width, g).start()

        each(A, send_stream)

    @pl.when(owner)
    def _():
        for g in range(G):
            @pl.when(mine * G + g != h)
            def _(g=g):
                copyr(g).wait_recv()
        for g in range(G):
            resf[g * S:(g + 1) * S, :] = recvr[g].astype(F32)
        groups(stream_step)

    sq[...] = jnp.zeros_like(sq)
    proj[...] = jnp.zeros_like(proj)
    tile_q = tile_of(Q, 768)

    def project_step(unit, width, g):
        all_landed(
            recv4.at[:, pl.ds(unit, width)], recv4.at[pl.ds(0, M - 1), pl.ds(unit, width)], r4.at[g]
        )
        for u in range(width):
            wq_copy(unit + u).wait()
            for m in range(M):
                rowsf[m * T:(m + 1) * T, u * C:(u + 1) * C] = recv4[m, unit + u].astype(F32)
        span = width * C
        wide = rowsf[:, :span]
        columns = pl.ds(pl.multiple_of(unit * C, C), span)
        for a in range(A):
            @pl.when(h == a)
            def _(a=a):
                ns_o[:, columns] = rowsf[a * S:(a + 1) * S, :span].astype(BF16)
        lhs2[:, :span] = (wide * gain[:, columns]).astype(BF16)
        sq[...] += jnp.sum(wide * wide, axis=1, keepdims=True)
        for n in range(0, Q, tile_q):
            proj[:, n:n + tile_q] += jnp.dot(
                lhs2[:, :span], wq[columns, n:n + tile_q], preferred_element_type=F32
            )

    groups(project_step)

    def copy5(t):
        d = lax.rem(r + t, B)
        return pltpu.make_async_remote_copy(
            src_ref=send5.at[d], dst_ref=recv5.at[r], send_sem=s5.at[t - 1],
            recv_sem=r5.at[t - 1], device_id={"row": d}, device_id_type=MESH,
        )

    for b in range(B):
        send5[b, :, :Q] = proj[b * Rl:(b + 1) * Rl, :]
        send5[b, :, Q:] = sq[b * Rl:(b + 1) * Rl, :]
    each(B, lambda t: copy5(t).start(), 1)
    recv5[r] = send5[r]

    all_landed(send1, send1.at[:, pl.ds(0, M - 1)], s1.at[0])
    all_landed(send3, send3.at[pl.ds(0, M - 1)], s3.at[0])

    @pl.when(home != h)
    def _():
        copyr(0).wait_send()

    @pl.when(owner)
    def _():
        landed(recv3.at[pl.ds(0, A - 1)], s4.at[0])
        for e in range(B):
            @pl.when(r == e)
            def _(e=e):
                landed(send2.at[:, pl.ds(0, A - 1)], s2.at[e])

            @pl.when(r != e)
            def _(e=e):
                landed(send2, s2.at[e])

    each(B, lambda t: copy5(t).wait(), 1)
    total = recv5[0]
    for b in range(1, B):
        total = total + recv5[b]
    inverse = lax.rsqrt(total[:, Q:Q + 1] / width_total + epsilon)
    out_o[...] = (
        total[:, :Q] * inverse * (qscale[...].astype(F32).reshape(1, Q) * 2.0 ** (-22))
    ).astype(BF16)


def hand_over(ns, out, ns_o, out_o, sem):
    first = pltpu.make_async_copy(ns, ns_o, sem.at[0])
    second = pltpu.make_async_copy(out, out_o, sem.at[1])
    first.start()
    second.start()
    first.wait()
    second.wait()


def body(gate, up, signs, wd, dscale, res, gain, wq, qscale):
    A = lax.axis_size("hid")
    B = lax.axis_size("row")
    N = A * B
    M = A // 2
    lo = (A - M) // 2
    Rl, FFl = gate.shape
    Dl = wd.shape[1]
    Q = wq.shape[1]
    R = Rl * B
    S = res.shape[0]
    q = Rl // M
    T = R // M
    J = 8 if Dl % (8 * 128) == 0 else 4
    C = Dl // J
    KC = 2
    L = FFl // KC
    any_spec = pl.BlockSpec(memory_space=pl.ANY)
    vmem_spec = pl.BlockSpec(memory_space=pltpu.VMEM)
    dma = pltpu.SemaphoreType.DMA
    call = pl.pallas_call(
        functools.partial(kernel, A, B, J, KC, J // 2 - 1, M, lo, Dl * B),
        out_shape=(pltpu.VMEM((S, Dl), BF16), pltpu.VMEM((Rl, Q), BF16)),
        in_specs=[any_spec] * 9,
        out_specs=(vmem_spec, vmem_spec),
        scratch_shapes=[
            pltpu.VMEM((Rl, FFl), BF16),
            pltpu.VMEM((Rl, FFl), BF16),
            pltpu.VMEM((1, FFl), jnp.int32),
            pltpu.VMEM((1, Dl), jnp.int32),
            pltpu.VMEM((S, Dl), BF16),
            pltpu.VMEM((Dl,), BF16),
            pltpu.VMEM((Q,), jnp.int32),
            pltpu.VMEM((J, FFl, C), BF16),
            pltpu.VMEM((Dl, Q), BF16),
            pltpu.VMEM((1, Dl), F32),
            pltpu.VMEM((KC, M, q, L), BF16),
            pltpu.VMEM((KC, A, q, L), BF16),
            pltpu.VMEM((A // M, S, Dl), BF16),
            pltpu.VMEM((T, Dl), F32),
            pltpu.VMEM((KC, A, q, L), BF16),
            pltpu.VMEM((KC, M * B, q, L), BF16),
            pltpu.VMEM((R, L), F32),
            pltpu.VMEM((R, FFl), BF16),
            pltpu.VMEM((M, J, T, C), BF16),
            pltpu.VMEM((A, J, T, C), BF16),
            pltpu.VMEM((J, T, C), BF16),
            pltpu.VMEM((M, J, T, C), BF16),
            pltpu.VMEM((R, 2 * C), F32),
            pltpu.VMEM((R, 2 * C), BF16),
            pltpu.VMEM((R, 128), F32),
            pltpu.VMEM((R, Q), F32),
            pltpu.VMEM((2, R, C), F32),
            pltpu.VMEM((B, Rl, Q + 128), F32),
            pltpu.VMEM((B, Rl, Q + 128), F32),
            dma((7,)),
            dma((J,)),
            dma((J,)),
            dma((1,)),
            dma((KC,)),
            dma((1,)),
            dma((A // M,)),
            dma((B,)),
            dma((KC,)),
            dma((1,)),
            dma((J // 2 + 1,)),
            dma((1,)),
            dma((J // 2 + 1,)),
            dma((B - 1,)),
            dma((B - 1,)),
        ],
        compiler_params=pltpu.CompilerParams(
            collective_id=0, has_side_effects=True, vmem_limit_bytes=62 * 1024 * 1024
        ),
    )
    made = call(
        gate, up, signs.reshape(1, -1), wd, dscale.reshape(1, -1), res, gain, wq,
        qscale,
    )
    return pl.pallas_call(
        hand_over,
        out_shape=(jax.ShapeDtypeStruct((S, Dl), BF16), jax.ShapeDtypeStruct((Rl, Q), BF16)),
        in_specs=[vmem_spec, vmem_spec],
        out_specs=(any_spec, any_spec),
        scratch_shapes=[dma((2,))],
    )(*(pltpu.with_memory_space_constraint(part, pltpu.VMEM) for part in made))


def solution(mesh):
    return jax.shard_map(
        body,
        mesh=mesh,
        in_specs=(
            P(("groups", "row"), "hid"),
            P(("groups", "row"), "hid"),
            P("hid"),
            P("hid", "row"),
            P("row"),
            P(("groups", "hid"), "row"),
            P("row"),
            P("row", "hid"),
            P("hid"),
        ),
        out_specs=(P(("groups", "hid"), "row"), P(("groups", "row"), "hid")),
        check_vma=False,
    )
```
